32 devices in a mesh: dp: 4 (over y, x), tensor: 8 (over z, core).
Axes of the slice: x: 2, y: 2, z: 4, core: 2. Of those that a mesh axis runs over, the one named last changes fastest.
Arguments:
- tokens: bfloat16 [2, 6144, 2048], P(None, ('dp', 'tensor')), may hold values from -6 to 6
- cotangent: bfloat16 [2, 6144, 2048], P(None, ('dp', 'tensor')), may hold values from -6 to 6
- lengths: int32 [2, 4, 6], P(None, 'dp'), may hold values from 1 to 1024, 1536 in all within a row
- places: int32 [2, 4, 1536], P(None, 'dp'), may hold values from 0 to 1535, each once within a row
- owners: int32 [4, 4], replicated, may hold values from 0 to 3, each once within a row
- qkv_weight: float32 [3, 2048, 2048], P(None, 'dp', 'tensor'), may hold values from -0.1875 to 0.1875
- qkv_first: float32 [3, 2048, 2048], P(None, 'dp', 'tensor'), may hold values from -1280 to 1280
- qkv_second: float32 [3, 2048, 2048], P(None, 'dp', 'tensor'), may hold values from 49152 to 196608
- out_weight: float32 [2048, 2048], P('tensor', 'dp'), may hold values from -0.375 to 0.375
- out_first: float32 [2048, 2048], P('tensor', 'dp'), may hold values from -320 to 320
- out_second: float32 [2048, 2048], P('tensor', 'dp'), may hold values from 3072 to 12288
- proj_weight: float32 [2, 2048, 8192], P(None, 'dp', 'tensor'), may hold values from -0.125 to 0.125
- proj_first: float32 [2, 2048, 8192], P(None, 'dp', 'tensor'), may hold values from -192 to 192
- proj_second: float32 [2, 2048, 8192], P(None, 'dp', 'tensor'), may hold values from 1105.92 to 4423.68
- down_weight: float32 [8192, 2048], P('tensor', 'dp'), may hold values from -0.0625 to 0.0625
- down_first: float32 [8192, 2048], P('tensor', 'dp'), may hold values from -384 to 384
- down_second: float32 [8192, 2048], P('tensor', 'dp'), may hold values from 4423.68 to 17694.72
Outputs:
- output: bfloat16 [2, 6144, 2048], P(None, ('dp', 'tensor'))
- input_grad: float32 [2, 6144, 2048], P(None, ('dp', 'tensor'))
- qkv_grad: float32 [3, 2048, 2048], P(None, 'dp', 'tensor')
- qkv_first_next: float32 [3, 2048, 2048], P(None, 'dp', 'tensor')
- qkv_second_next: float32 [3, 2048, 2048], P(None, 'dp', 'tensor')
- qkv_master: float32 [3, 2048, 2048], P(None, 'dp', 'tensor')
- out_grad: float32 [2048, 2048], P('tensor', 'dp')
- out_first_next: float32 [2048, 2048], P('tensor', 'dp')
- out_second_next: float32 [2048, 2048], P('tensor', 'dp')
- out_master: float32 [2048, 2048], P('tensor', 'dp')
- proj_grad: float32 [2, 2048, 8192], P(None, 'dp', 'tensor')
- proj_first_next: float32 [2, 2048, 8192], P(None, 'dp', 'tensor')
- proj_second_next: float32 [2, 2048, 8192], P(None, 'dp', 'tensor')
- proj_master: float32 [2, 2048, 8192], P(None, 'dp', 'tensor')
- down_grad: float32 [8192, 2048], P('tensor', 'dp')
- down_first_next: float32 [8192, 2048], P('tensor', 'dp')
- down_second_next: float32 [8192, 2048], P('tensor', 'dp')
- down_master: float32 [8192, 2048], P('tensor', 'dp')
The draws below stay inside these ranges and needn't reach their ends.
Inputs may be any that keep to these rules, and one draw needn't show every extreme that they name: Each row of 6 lengths sums to 1536 and its largest is exactly 1024. `places`: each row names every place of its group once. `owners`: each row names every block once.
All inputs are finite; a program needn't handle non-finite values.
Results may differ from the reference program's by a relative error of at most 0.02.
Values may be sent and summed in bfloat16 or wider, within the bound.
No kernel may reach another device: no remote copies, remote signals or barrier semaphores. Data moves between devices by JAX's collectives and lax.ppermute only.
A program may use at most 320 MiB of HBM per device.

```python
import math
import jax
import jax.numpy as jnp
import numpy as np
from jax import lax

H = 16
HD = 128
D = 2048
FF = 8192
TG = 1536
NSEQ = 6
M = 2
MOST = 1024
TOKENS = 6144
QB = 512
N_DP = 4


def level_of(key, shape, cuts, low, high):
    gain, own = 1.0, jax.random.fold_in(key, 6)
    for axis_at, shards_of in cuts:
        steps = jnp.exp(jax.random.uniform(jax.random.fold_in(own, axis_at), (shards_of,), jnp.float32, low / len(cuts), high / len(cuts)))
        gain = gain * jnp.repeat(steps, shape[axis_at] // shards_of).reshape([-1 if axis == axis_at else 1 for axis in range(len(shape))])
    return gain


def split_up(number_of, total, reach, slope):
    weights = [(1 << 20) // math.isqrt(standing ** slope) + 1 for standing in range(2, number_of + 1)]
    spare, counts = total - reach - (number_of - 1), [1] * (number_of - 1)
    while spare > 0:
        movable = [i for i in range(number_of - 1) if counts[i] < reach]
        pool, left = sum([weights[i] for i in movable]), spare
        for i in movable:
            extra = min(reach - counts[i], max(1, left * weights[i] // pool), spare)
            counts[i] = counts[i] + extra
            spare = spare - extra
    return np.array([reach] + counts)


def uneven_parts(own_key, number_of, total, limit, skew):
    if number_of == 2:
        one = jax.random.randint(own_key, (), max(1, total - limit), min(limit, total - 1) + 1)
        return jnp.stack([one, total - one])
    sizes = jnp.asarray(split_up(number_of, total, limit, skew), jnp.int32)
    pairs = (number_of - 1) // 2
    source_of, taker = sizes[1:1 + 2 * pairs:2], sizes[2:2 + 2 * pairs:2]
    slack = jnp.minimum(source_of - 1, limit - taker)
    moved = jax.random.randint(jax.random.fold_in(own_key, 1), (pairs,), 0, 1 << 20) % (slack + 1)
    sizes = sizes.at[1:1 + 2 * pairs:2].set(source_of - moved).at[2:2 + 2 * pairs:2].set(taker + moved)
    return sizes[jax.random.permutation(jax.random.fold_in(own_key, 2), number_of)]


def gaussian(stream_key, extent, scale, reach, pieces=(), held_as=jnp.bfloat16):
    gain = level_of(stream_key, extent, pieces, -0.22, 0.18) if pieces else 1.0
    drawn = jax.random.normal(stream_key, extent, jnp.float32) * scale * gain
    return jnp.minimum(jnp.maximum(drawn, -reach), reach).astype(held_as)


def setup_inputs(seed: int = 0) -> dict:
    key_list = jax.random.split(jax.random.key(seed), 18)
    return {
        "tokens": gaussian(key_list[0], (M, TOKENS, D), 1.0, 6.0, ((1, 32),)),
        "cotangent": gaussian(key_list[1], (M, TOKENS, D), 1.0, 6.0, ((1, 32),)),
        "lengths": jax.vmap(lambda own: uneven_parts(own, NSEQ, TG, MOST, 2))(jax.random.split(key_list[2], M * N_DP)).reshape((M, N_DP, NSEQ)).astype(jnp.int32),
        "places": jax.vmap(lambda own: jax.random.permutation(own, TG))(jax.random.split(key_list[3], M * N_DP)).reshape((M, N_DP, TG)).astype(jnp.int32),
        "owners": jax.vmap(lambda own: jax.random.permutation(own, N_DP))(jax.random.split(key_list[4], 4)).reshape((4, N_DP)).astype(jnp.int32),
        "qkv_weight": gaussian(key_list[5], (3, D, D), (D // 2) ** -0.5, 0.1875, ((1, 4), (2, 8)), jnp.float32),
        "qkv_first": gaussian(key_list[6], (3, D, D), (2 * (M * TOKENS) ** 0.5), 1280.0, ((1, 4), (2, 8)), jnp.float32),
        "qkv_second": jnp.clip(jnp.exp(math.log(196608.0) - 1.3862944 * jax.random.uniform(key_list[7], (3, D, D), jnp.float32) ** level_of(key_list[7], (3, D, D), ((1, 4), (2, 8)), -0.2, 0.2)), 49152.0, 196608.0),
        "out_weight": gaussian(key_list[8], (D, D), (D // 8) ** -0.5, 0.375, ((0, 8), (1, 4)), jnp.float32),
        "out_first": gaussian(key_list[9], (D, D), (0.5 * (M * TOKENS) ** 0.5), 320.0, ((0, 8), (1, 4)), jnp.float32),
        "out_second": jnp.clip(jnp.exp(math.log(12288.0) - 1.3862944 * jax.random.uniform(key_list[10], (D, D), jnp.float32) ** level_of(key_list[10], (D, D), ((0, 8), (1, 4)), -0.2, 0.2)), 3072.0, 12288.0),
        "proj_weight": gaussian(key_list[11], (2, D, FF), D ** -0.5, 0.125, ((1, 4), (2, 8)), jnp.float32),
        "proj_first": gaussian(key_list[12], (2, D, FF), (0.3 * (M * TOKENS) ** 0.5), 192.0, ((1, 4), (2, 8)), jnp.float32),
        "proj_second": jnp.clip(jnp.exp(math.log(4423.68) - 1.3862944 * jax.random.uniform(key_list[13], (2, D, FF), jnp.float32) ** level_of(key_list[13], (2, D, FF), ((1, 4), (2, 8)), -0.2, 0.2)), 1105.92, 4423.68),
        "down_weight": gaussian(key_list[14], (FF, D), FF ** -0.5, 0.0625, ((0, 8), (1, 4)), jnp.float32),
        "down_first": gaussian(key_list[15], (FF, D), (0.6 * (M * TOKENS) ** 0.5), 384.0, ((0, 8), (1, 4)), jnp.float32),
        "down_second": jnp.clip(jnp.exp(math.log(17694.72) - 1.3862944 * jax.random.uniform(key_list[16], (FF, D), jnp.float32) ** level_of(key_list[16], (FF, D), ((0, 8), (1, 4)), -0.2, 0.2)), 4423.68, 17694.72),
    }


@jax.custom_vjp
def low(v):
    return lax.optimization_barrier(v.astype(jnp.bfloat16)).astype(jnp.float32)

@jax.custom_vjp
def low_back(v):
    return v

def low_keep(v):
    return (low(v), None)

def low_pass(kept, grad):
    return (grad,)

def back_keep(v):
    return (v, None)

def back_low(kept, grad):
    return (low(grad),)
low.defvjp(low_keep, low_pass)
low_back.defvjp(back_keep, back_low)
HIGHEST = lax.Precision.HIGHEST
RATES = (0.03, 0.06, 0.02, 0.01)

def inverse_order(order):
    count = order.shape[0]
    return jnp.zeros((count,), jnp.int32).at[order].set(jnp.arange(count, dtype=jnp.int32))

def reorder_blocks(weight, order):
    shape = weight.shape
    split = shape[:1] + (order.shape[0], shape[1] // order.shape[0]) + shape[2:]
    return jnp.take(weight.reshape(split), order, axis=1).reshape(shape)

def normalize(values):
    center = values - lax.optimization_barrier(jnp.mean(values, axis=-1, keepdims=True))
    return center * lax.rsqrt(lax.optimization_barrier(jnp.mean(center * center, axis=-1, keepdims=True)) + 1e-05)

def rotate(values, cosine, sine):
    half = values.shape[-1] // 2
    first = values[..., :half]
    second = values[..., half:]
    return jnp.concatenate([first * cosine - second * sine, second * cosine + first * sine], axis=-1)

def layout(lengths, count, head_size):
    place = jnp.arange(count, dtype=jnp.int32)
    ends = jnp.cumsum(lengths).astype(jnp.int32)
    starts = (ends - lengths).astype(jnp.int32)
    segment = lax.optimization_barrier(jnp.sum((place[:, None] >= ends[None, :]).astype(jnp.int32), axis=1)).astype(jnp.int32)
    begin = lax.optimization_barrier(jnp.max(jnp.where(starts[None, :] <= place[:, None], starts[None, :], 0), axis=1)).astype(jnp.int32)
    position = (place - begin).astype(jnp.float32)
    half = head_size // 2
    freq = jnp.exp(jnp.arange(half, dtype=jnp.float32) * (-2.0 * math.log(10000.0) / head_size))
    angle = position[:, None] * freq[None, :]
    return (segment, place, jnp.cos(angle), jnp.sin(angle))

def attend(query, keys, values, segment, place):
    blocks = TG // QB
    stacked = query.reshape(H, blocks, QB, HD).transpose(1, 0, 2, 3)
    seg_rows = segment.reshape(blocks, QB)
    place_rows = place.reshape(blocks, QB)
    scale = HD ** (-0.5)

    def one_block(item):
        query_block, seg_block, place_block = item
        scores = low_back(jnp.einsum('hqd,hkd->hqk', query_block, keys, precision=HIGHEST) * scale)
        allowed = (seg_block[:, None] == segment[None, :]) & (place[None, :] <= place_block[:, None])
        scores = jnp.where(allowed[None], scores, -1e+30)
        top = lax.optimization_barrier(jnp.max(scores, axis=-1, keepdims=True))
        expo = jnp.exp(scores - top)
        probs = expo / lax.optimization_barrier(jnp.sum(expo, axis=-1, keepdims=True))
        return jnp.einsum('hqk,hkd->hqd', low(probs), values, precision=HIGHEST)
    result = lax.map(jax.checkpoint(one_block), (stacked, seg_rows, place_rows))
    return result.transpose(1, 0, 2, 3).reshape(H, TG, HD)

def layer(rows_in, w_qkv, w_out, w_proj, w_down, segment, place, cosine, sine, order, back):
    w_qkv = low(w_qkv)
    w_out = low(w_out)
    w_proj = low(w_proj)
    w_down = low(w_down)
    normed = low(normalize(rows_in))[order]
    joined = low_back(jnp.einsum('td,sde->ste', normed, w_qkv, precision=HIGHEST))
    heads = joined.reshape(3, TG, H, HD).transpose(0, 2, 1, 3)
    query = low(rotate(heads[0], cosine, sine))
    keys = low(rotate(heads[1], cosine, sine))
    values = low(heads[2])
    attended = low(low_back(attend(query, keys, values, segment, place)))
    attn_rows = attended.transpose(1, 0, 2).reshape(TG, D)
    branch_one = low_back(jnp.dot(attn_rows, w_out, precision=HIGHEST)[back])
    middle = rows_in + branch_one
    normed_two = low(normalize(middle))
    gate_up = low_back(jnp.einsum('td,sdf->stf', normed_two, w_proj, precision=HIGHEST))
    hidden = low(jax.nn.silu(gate_up[0]) * gate_up[1])
    branch_two = low_back(jnp.dot(hidden, w_down, precision=HIGHEST))
    return middle + branch_two

def adamw(master, first, second, grad, rate):
    first_next = 0.5 * first + 0.5 * grad
    second_next = 0.5 * second + 0.5 * grad * grad
    master_next = master - rate * (first_next / (jnp.sqrt(second_next) + 1e-08) + 0.1 * master)
    return (grad, first_next, second_next, master_next)

def reference(tokens, cotangent, lengths, places, owners, qkv_weight, qkv_first, qkv_second, out_weight, out_first, out_second, proj_weight, proj_first, proj_second, down_weight, down_first, down_second):
    masters = (qkv_weight, out_weight, proj_weight, down_weight)
    logical = tuple((reorder_blocks(masters[index], inverse_order(owners[index])) for index in range(4)))
    groups = M * N_DP
    rows_all = tokens.reshape(groups, TG, D)
    cot_all = cotangent.reshape(groups, TG, D)
    len_all = lengths.reshape(groups, NSEQ)
    place_all = places.reshape(groups, TG)

    def step(carry, item):
        rows_in, cot_rows, seq_lengths, order = item
        segment, place, cosine, sine = layout(seq_lengths, TG, HD)
        back = inverse_order(order)

        def forward(rows_value, w_qkv, w_out, w_proj, w_down):
            return layer(rows_value, w_qkv, w_out, w_proj, w_down, segment, place, cosine, sine, order, back)
        result, pullback = jax.vjp(forward, rows_in.astype(jnp.float32), *logical)
        grads = pullback(cot_rows.astype(jnp.float32))
        carry = tuple((running + current for running, current in zip(carry, grads[1:])))
        return (carry, (result.astype(jnp.bfloat16), grads[0]))
    start = tuple((jnp.zeros(weight.shape, jnp.float32) for weight in logical))
    totals, (outputs, input_grads) = lax.scan(step, start, (rows_all, cot_all, len_all, place_all))
    output = outputs.reshape(M, TOKENS, D)
    input_grad = input_grads.reshape(M, TOKENS, D)
    stored = tuple((reorder_blocks(totals[index], owners[index]) for index in range(4)))
    qkv_new = adamw(qkv_weight, qkv_first, qkv_second, stored[0], RATES[0])
    out_new = adamw(out_weight, out_first, out_second, stored[1], RATES[1])
    proj_new = adamw(proj_weight, proj_first, proj_second, stored[2], RATES[2])
    down_new = adamw(down_weight, down_first, down_second, stored[3], RATES[3])
    return (output, input_grad, qkv_new[0], qkv_new[1], qkv_new[2], qkv_new[3], out_new[0], out_new[1], out_new[2], out_new[3], proj_new[0], proj_new[1], proj_new[2], proj_new[3], down_new[0], down_new[1], down_new[2], down_new[3])
```

```python
import math

import jax
import jax.numpy as jnp
from jax import lax
from jax.experimental import pallas as pl
from jax.experimental.pallas import tpu as pltpu
from jax.sharding import PartitionSpec as P

HD = 128
RATES = (0.03, 0.06, 0.02, 0.01)
NEG = -1e30
ROW_COMM = "pp"


def inverse_order(order):
    count = order.shape[0]
    hit = order[None, :] == jnp.arange(count, dtype=jnp.int32)[:, None]
    return jnp.sum(jnp.where(hit, jnp.arange(count, dtype=jnp.int32)[None, :], 0), axis=1)


def pick_blocks(values, order):
    count = order.shape[0]
    width = values.shape[1] // count
    blocks = [values[:, j * width : (j + 1) * width] for j in range(count)]
    picked = []
    for k in range(count):
        chosen = blocks[0]
        for j in range(1, count):
            chosen = jnp.where(order[k] == j, blocks[j], chosen)
        picked.append(chosen)
    return jnp.concatenate(picked, axis=1)


def normalize(values):
    center = values - jnp.mean(values, axis=-1, keepdims=True)
    scale = lax.rsqrt(jnp.mean(center * center, axis=-1, keepdims=True) + 1e-05)
    return (center * scale, scale)


def normalize_back(normed, scale, grad):
    return scale * (
        grad
        - jnp.mean(grad, axis=-1, keepdims=True)
        - normed * jnp.mean(grad * normed, axis=-1, keepdims=True)
    )


def layout(lengths, place, head_size):
    ends = jnp.cumsum(lengths)
    starts = ends - lengths
    begin = jnp.max(jnp.where(starts[None, :] <= place[:, None], starts[None, :], 0), axis=1)
    position = (place - begin).astype(jnp.float32)
    half = head_size // 2
    freq = jnp.exp(jnp.arange(half, dtype=jnp.float32) * (-2.0 * math.log(10000.0) / head_size))
    angle = position[:, None] * freq[None, :]
    cosine, sine = jnp.cos(angle), jnp.sin(angle)
    return (
        begin,
        jnp.concatenate([cosine, cosine], axis=1),
        jnp.concatenate([-sine, sine], axis=1),
    )


def spin(values, cosine, sine):
    return values * cosine + pltpu.roll(values, HD // 2, 1) * sine


def attend_kernel(
    q_ref, k_ref, v_ref, cq_ref, sq_ref, ck_ref, sk_ref, pq_ref, bq_ref, pk_ref,
    o_ref, lse_ref, saved_ref,
):
    step = pl.program_id(1)
    rows = q_ref.shape[1]
    factor = HD ** (-0.5) * math.log2(math.e)

    @pl.when(step == 0)
    def _():
        saved_ref[1] = spin(k_ref[0], ck_ref[...], sk_ref[...]).astype(jnp.bfloat16)
        saved_ref[2] = v_ref[0].astype(jnp.bfloat16)

    query = spin(q_ref[0], cq_ref[...], sq_ref[...]).astype(jnp.bfloat16)
    saved_ref[0, pl.ds(step * rows, rows), :] = query
    scores = lax.dot_general(
        query, saved_ref[1], (((1,), (1,)), ((), ())), preferred_element_type=jnp.float32
    )
    place = pk_ref[...]
    allowed = (place <= pq_ref[...]) & (place >= bq_ref[...])
    scores = jnp.where(allowed, scores * factor, NEG)
    top = jnp.max(scores, axis=1, keepdims=True)
    expo = jnp.exp2(scores - top)
    total = jnp.sum(expo, axis=1, keepdims=True)
    result = jnp.dot(
        expo.astype(jnp.bfloat16), saved_ref[2], preferred_element_type=jnp.float32
    )
    o_ref[...] = (result / total).astype(jnp.bfloat16)
    lse_ref[0] = top + jnp.log2(total)


def attend(joined, place, begin, cosine, sine):
    _, count, cols = joined.shape
    rows = min(512, count)
    heads = cols // HD
    return pl.pallas_call(
        attend_kernel,
        name="attend",
        grid=(heads, count // rows),
        in_specs=[
            pl.BlockSpec((1, rows, HD), lambda h, i: (0, i, h)),
            pl.BlockSpec((1, count, HD), lambda h, i: (1, 0, h)),
            pl.BlockSpec((1, count, HD), lambda h, i: (2, 0, h)),
            pl.BlockSpec((rows, HD), lambda h, i: (i, 0)),
            pl.BlockSpec((rows, HD), lambda h, i: (i, 0)),
            pl.BlockSpec((count, HD), lambda h, i: (0, 0)),
            pl.BlockSpec((count, HD), lambda h, i: (0, 0)),
            pl.BlockSpec((rows, 1), lambda h, i: (i, 0)),
            pl.BlockSpec((rows, 1), lambda h, i: (i, 0)),
            pl.BlockSpec((1, count), lambda h, i: (0, 0)),
        ],
        out_specs=[
            pl.BlockSpec((rows, HD), lambda h, i: (i, h)),
            pl.BlockSpec((1, rows, 1), lambda h, i: (h, i, 0)),
            pl.BlockSpec((3, count, HD), lambda h, i: (0, 0, h)),
        ],
        out_shape=[
            jax.ShapeDtypeStruct((count, cols), jnp.bfloat16),
            jax.ShapeDtypeStruct((heads, count, 1), jnp.float32),
            jax.ShapeDtypeStruct((3, count, cols), jnp.bfloat16),
        ],
        compiler_params=pltpu.CompilerParams(vmem_limit_bytes=56 * 1024 * 1024),
        cost_estimate=pl.CostEstimate(
            flops=4 * count * count * cols,
            transcendentals=heads * count * count,
            bytes_accessed=24 * count * cols,
        ),
    )(
        joined, joined, joined, cosine, sine, cosine, sine,
        place[:, None], begin[:, None], place[None, :],
    )


def attend_back_kernel(
    saved_q_ref, saved_k_ref, saved_v_ref, g_ref, lse_ref, cq_ref, sq_ref, ck_ref, sk_ref,
    pq_ref, bq_ref, pk_ref, out_ref, dk_ref, dv_ref,
):
    step = pl.program_id(1)
    rows = saved_q_ref.shape[1]
    scale = HD ** (-0.5)
    factor = scale * math.log2(math.e)

    @pl.when(step == 0)
    def _():
        dk_ref[...] = jnp.zeros_like(dk_ref)
        dv_ref[...] = jnp.zeros_like(dv_ref)

    query = saved_q_ref[0]
    keys = saved_k_ref[0]
    grad = g_ref[...]
    scores = lax.dot_general(
        query, keys, (((1,), (1,)), ((), ())), preferred_element_type=jnp.float32
    )
    place = pk_ref[...]
    allowed = (place <= pq_ref[...]) & (place >= bq_ref[...])
    probs = jnp.exp2(jnp.where(allowed, scores * factor, NEG) - lse_ref[0])
    grad_probs = lax.dot_general(
        grad, saved_v_ref[0], (((1,), (1,)), ((), ())), preferred_element_type=jnp.float32
    )
    product = probs * grad_probs
    delta = jnp.sum(product, axis=1, keepdims=True)
    grad_scores = (product - probs * delta).astype(jnp.bfloat16)
    dv_ref[...] += lax.dot_general(
        probs.astype(jnp.bfloat16), grad, (((0,), (0,)), ((), ())),
        preferred_element_type=jnp.float32,
    )
    dk_ref[...] += lax.dot_general(
        grad_scores, query, (((0,), (0,)), ((), ())), preferred_element_type=jnp.float32
    )
    grad_query = jnp.dot(grad_scores, keys, preferred_element_type=jnp.float32) * scale
    out_ref[0, pl.ds(step * rows, rows), :] = spin(
        grad_query, cq_ref[...], -sq_ref[...]
    ).astype(jnp.bfloat16)

    @pl.when(step == pl.num_programs(1) - 1)
    def _():
        out_ref[1] = spin(dk_ref[...] * scale, ck_ref[...], -sk_ref[...]).astype(jnp.bfloat16)
        out_ref[2] = dv_ref[...].astype(jnp.bfloat16)


def attend_back(saved, grad, lse, place, begin, cosine, sine):
    _, count, cols = saved.shape
    rows = min(512, count)
    heads = cols // HD
    return pl.pallas_call(
        attend_back_kernel,
        name="attend_back",
        grid=(heads, count // rows),
        in_specs=[
            pl.BlockSpec((1, rows, HD), lambda h, i: (0, i, h)),
            pl.BlockSpec((1, count, HD), lambda h, i: (1, 0, h)),
            pl.BlockSpec((1, count, HD), lambda h, i: (2, 0, h)),
            pl.BlockSpec((rows, HD), lambda h, i: (i, h)),
            pl.BlockSpec((1, rows, 1), lambda h, i: (h, i, 0)),
            pl.BlockSpec((rows, HD), lambda h, i: (i, 0)),
            pl.BlockSpec((rows, HD), lambda h, i: (i, 0)),
            pl.BlockSpec((count, HD), lambda h, i: (0, 0)),
            pl.BlockSpec((count, HD), lambda h, i: (0, 0)),
            pl.BlockSpec((rows, 1), lambda h, i: (i, 0)),
            pl.BlockSpec((rows, 1), lambda h, i: (i, 0)),
            pl.BlockSpec((1, count), lambda h, i: (0, 0)),
        ],
        out_specs=pl.BlockSpec((3, count, HD), lambda h, i: (0, 0, h)),
        out_shape=jax.ShapeDtypeStruct((3, count, cols), jnp.bfloat16),
        scratch_shapes=[
            pltpu.VMEM((count, HD), jnp.float32),
            pltpu.VMEM((count, HD), jnp.float32),
        ],
        compiler_params=pltpu.CompilerParams(vmem_limit_bytes=56 * 1024 * 1024),
        cost_estimate=pl.CostEstimate(
            flops=10 * count * count * cols,
            transcendentals=heads * count * count,
            bytes_accessed=24 * count * cols,
        ),
    )(
        saved, saved, saved, grad, lse, cosine, sine, cosine, sine,
        place[:, None], begin[:, None], place[None, :],
    )


def send(values, pairs):
    return lax.ppermute(values, "tensor", pairs)


def up_pairs(low, high):
    return [(2 * z + c, 2 * z + 2 + c) for z in range(low, high) for c in range(2)]


def down_pairs(low, high):
    return [(2 * z + c, 2 * z - 2 + c) for z in range(low, high) for c in range(2)]


def partner_pairs(size):
    return [(t, t ^ 1) for t in range(size)]


def row_order(size):
    if ROW_COMM == "sc":
        return jnp.arange(size, dtype=jnp.int32)
    mine = lax.axis_index("tensor")
    chips = size // 2
    chip, core = mine // 2, mine % 2
    chip_of = (chip - jnp.arange(chips, dtype=jnp.int32)) % chips
    return jnp.concatenate([chip_of * 2 + core, chip_of * 2 + 1 - core])


def gather_rows(rows, size):
    if ROW_COMM == "sc":
        return lax.all_gather(rows, "tensor", axis=0, tiled=True)
    chips = size // 2
    chip = lax.axis_index("tensor") // 2
    up, down = {}, {}
    going_up = going_down = rows
    for s in range(1, chips):
        going_up = up[s] = send(going_up, up_pairs(s - 1, chips - 1))
        going_down = down[s] = send(going_down, down_pairs(1, chips - s + 1))
    mine = [rows]
    for s in range(1, chips):
        mine.append(jnp.where(chip >= s, up[s], down[chips - s]))
    other = [send(piece, partner_pairs(size)) for piece in mine]
    return jnp.concatenate(mine + other, axis=0)


def scatter_rows(make, count, size):
    if ROW_COMM == "sc":
        return lax.psum_scatter(
            make(0, count).astype(jnp.bfloat16), "tensor", scatter_dimension=0, tiled=True
        ).astype(jnp.float32)
    chips = size // 2
    half = count // 2
    each = half // chips
    given = send(make(half, count).astype(jnp.bfloat16), partner_pairs(size))
    mine = (make(0, half) + given.astype(jnp.float32)).astype(jnp.bfloat16)
    piece = [mine[s * each : (s + 1) * each] for s in range(chips)]
    up = down = None
    for t in range(1, chips):
        going_up, going_down = piece[t], piece[chips - t]
        if up is not None:
            going_up = (going_up.astype(jnp.float32) + up).astype(jnp.bfloat16)
            going_down = (going_down.astype(jnp.float32) + down).astype(jnp.bfloat16)
        up = send(going_up, up_pairs(0, t)).astype(jnp.float32)
        down = send(going_down, down_pairs(chips - t, chips)).astype(jnp.float32)
    return piece[0].astype(jnp.float32) + up + down


def fetch(weight, axis):
    return lax.all_gather(weight.astype(jnp.bfloat16), "dp", axis=axis, tiled=True)


def reduce_owned(term):
    return lax.psum_scatter(
        term.astype(jnp.bfloat16), "dp", scatter_dimension=1, tiled=True
    ).astype(jnp.float32)


def adamw(master, first, second, grad, rate):
    first_next = 0.5 * first + 0.5 * grad
    second_next = 0.5 * second + 0.5 * grad * grad
    master_next = master - rate * (first_next / (jnp.sqrt(second_next) + 1e-08) + 0.1 * master)
    return (grad, first_next, second_next, master_next)


def body(
    tokens,
    cotangent,
    lengths,
    places,
    owners,
    qkv_weight,
    qkv_first,
    qkv_second,
    out_weight,
    out_first,
    out_second,
    proj_weight,
    proj_first,
    proj_second,
    down_weight,
    down_first,
    down_second,
):
    f32, bf16 = jnp.float32, jnp.bfloat16
    groups = tokens.shape[0]
    each_rows = tokens.shape[1]
    count = places.shape[2]
    size = count // each_rows
    back_owners = [inverse_order(owners[i]) for i in range(4)]
    w_qkv = fetch(qkv_weight, 1)
    w_out = fetch(out_weight, 1)
    w_proj = fetch(proj_weight, 1)
    w_down = fetch(down_weight, 1)
    order_of_rows = row_order(size)

    place, begin, cosine, sine = [], [], [], []
    rows_in, normed_one, scale_one, rows_a, grads_two = [], [], [], [], []
    for m in range(groups):
        arrival = inverse_order(places[m, 0])
        mine = jnp.take(arrival.reshape(size, each_rows), order_of_rows, axis=0).reshape(-1)
        first, cos, sin = layout(lengths[m, 0], mine, HD)
        place.append(mine)
        begin.append(first)
        cosine.append(cos)
        sine.append(sin)
        rows_in.append(tokens[m].astype(f32))
        normed, scale = normalize(rows_in[m])
        normed_one.append(normed)
        scale_one.append(scale)
        rows_a.append(gather_rows(pick_blocks(normed.astype(bf16), owners[0]), size))
    for m in range(groups):
        grads_two.append(gather_rows(pick_blocks(cotangent[m], owners[3]), size))

    outputs, input_grads = [], []
    total = None
    state = []
    for m in range(groups):
        joined = jnp.einsum("td,sdc->stc", rows_a[m], w_qkv, preferred_element_type=f32)
        attended, lse, saved = attend(joined, place[m], begin[m], cosine[m], sine[m])
        branch_one = scatter_rows(
            lambda low, high, attended=attended: jnp.dot(
                attended[low:high], w_out, preferred_element_type=f32
            ),
            count,
            size,
        )
        middle = rows_in[m] + pick_blocks(branch_one, back_owners[1])
        normed_two, scale_two = normalize(middle)
        rows_b = gather_rows(pick_blocks(normed_two.astype(bf16), owners[2]), size)
        gate_up = jnp.einsum("td,sdf->stf", rows_b, w_proj, preferred_element_type=f32)
        sigma = jax.nn.sigmoid(gate_up[0])
        activated = gate_up[0] * sigma
        hidden = (activated * gate_up[1]).astype(bf16)
        branch_two = scatter_rows(
            lambda low, high, hidden=hidden: jnp.dot(
                hidden[low:high], w_down, preferred_element_type=f32
            ),
            count,
            size,
        )
        outputs.append((middle + pick_blocks(branch_two, back_owners[3])).astype(bf16))
        term_down = jnp.einsum("tf,td->fd", hidden, grads_two[m], preferred_element_type=f32)
        grad_hidden = jnp.einsum("td,fd->tf", grads_two[m], w_down, preferred_element_type=f32)
        grad_gate = grad_hidden * gate_up[1] * sigma * (1.0 + gate_up[0] * (1.0 - sigma))
        grad_up = grad_hidden * activated
        grad_gate_up = jnp.stack([grad_gate, grad_up]).astype(bf16)
        term_proj = jnp.einsum("td,stf->sdf", rows_b, grad_gate_up, preferred_element_type=f32)
        grad_normed_two = pick_blocks(
            scatter_rows(
                lambda low, high, g=grad_gate_up: jnp.einsum(
                    "stf,sdf->td", g[:, low:high], w_proj, preferred_element_type=f32
                ),
                count,
                size,
            ),
            back_owners[2],
        )
        grad_middle = cotangent[m].astype(f32) + normalize_back(
            normed_two, scale_two, grad_normed_two
        )
        grads_one = gather_rows(pick_blocks(grad_middle.astype(bf16), owners[1]), size)
        term_out = jnp.einsum("tc,td->cd", attended, grads_one, preferred_element_type=f32)
        grad_attn = jnp.einsum("td,cd->tc", grads_one, w_out, preferred_element_type=f32)
        grad_joined = attend_back(
            saved, grad_attn.astype(bf16), lse, place[m], begin[m], cosine[m], sine[m]
        )
        term_qkv = jnp.einsum("td,stc->sdc", rows_a[m], grad_joined, preferred_element_type=f32)
        grad_normed_one = pick_blocks(
            scatter_rows(
                lambda low, high, g=grad_joined: jnp.einsum(
                    "stc,sdc->td", g[:, low:high], w_qkv, preferred_element_type=f32
                ),
                count,
                size,
            ),
            back_owners[0],
        )
        input_grads.append(
            grad_middle + normalize_back(normed_one[m], scale_one[m], grad_normed_one)
        )
        terms = (term_qkv, term_out, term_proj, term_down)
        total = terms if total is None else tuple(a + b for a, b in zip(total, terms))
    down_new = adamw(down_weight, down_first, down_second, reduce_owned(total[3]), RATES[3])
    proj_new = adamw(proj_weight, proj_first, proj_second, reduce_owned(total[2]), RATES[2])
    out_new = adamw(out_weight, out_first, out_second, reduce_owned(total[1]), RATES[1])
    qkv_new = adamw(qkv_weight, qkv_first, qkv_second, reduce_owned(total[0]), RATES[0])
    return (
        jnp.stack(outputs),
        jnp.stack(input_grads),
        *qkv_new,
        *out_new,
        *proj_new,
        *down_new,
    )


def solution(mesh):
    placed = (
        P(None, ("dp", "tensor"), None),
        P(None, ("dp", "tensor"), None),
        P(None, "dp", None),
        P(None, "dp", None),
        P(),
        P(None, "dp", "tensor"),
        P(None, "dp", "tensor"),
        P(None, "dp", "tensor"),
        P("tensor", "dp"),
        P("tensor", "dp"),
        P("tensor", "dp"),
        P(None, "dp", "tensor"),
        P(None, "dp", "tensor"),
        P(None, "dp", "tensor"),
        P("tensor", "dp"),
        P("tensor", "dp"),
        P("tensor", "dp"),
    )
    return jax.shard_map(
        body,
        mesh=mesh,
        in_specs=placed,
        out_specs=(
            P(None, ("dp", "tensor"), None),
            P(None, ("dp", "tensor"), None),
            P(None, "dp", "tensor"),
            P(None, "dp", "tensor"),
            P(None, "dp", "tensor"),
            P(None, "dp", "tensor"),
            P("tensor", "dp"),
            P("tensor", "dp"),
            P("tensor", "dp"),
            P("tensor", "dp"),
            P(None, "dp", "tensor"),
            P(None, "dp", "tensor"),
            P(None, "dp", "tensor"),
            P(None, "dp", "tensor"),
            P("tensor", "dp"),
            P("tensor", "dp"),
            P("tensor", "dp"),
            P("tensor", "dp"),
        ),
        check_vma=False,
    )
```

```python
import math

import jax
import jax.numpy as jnp
from jax import lax
from jax.experimental import pallas as pl
from jax.experimental.pallas import tpu as pltpu
from jax.sharding import PartitionSpec as P

HD = 128
RATES = (0.03, 0.06, 0.02, 0.01)
NEG = -1e30
ROW_COMM = ("pp", "pp")


def inverse_order(order):
    count = order.shape[0]
    hit = order[None, :] == jnp.arange(count, dtype=jnp.int32)[:, None]
    return jnp.sum(jnp.where(hit, jnp.arange(count, dtype=jnp.int32)[None, :], 0), axis=1)


def pick_blocks(values, order):
    count = order.shape[0]
    width = values.shape[1] // count
    blocks = [values[:, j * width : (j + 1) * width] for j in range(count)]
    picked = []
    for k in range(count):
        chosen = blocks[0]
        for j in range(1, count):
            chosen = jnp.where(order[k] == j, blocks[j], chosen)
        picked.append(chosen)
    return jnp.concatenate(picked, axis=1)


def normalize(values):
    center = values - jnp.mean(values, axis=-1, keepdims=True)
    scale = lax.rsqrt(jnp.mean(center * center, axis=-1, keepdims=True) + 1e-05)
    return (center * scale, scale)


def normalize_back(normed, scale, grad):
    return scale * (
        grad
        - jnp.mean(grad, axis=-1, keepdims=True)
        - normed * jnp.mean(grad * normed, axis=-1, keepdims=True)
    )


def layout(lengths, place, head_size):
    ends = jnp.cumsum(lengths)
    starts = ends - lengths
    begin = jnp.max(jnp.where(starts[None, :] <= place[:, None], starts[None, :], 0), axis=1)
    position = (place - begin).astype(jnp.float32)
    half = head_size // 2
    freq = jnp.exp(jnp.arange(half, dtype=jnp.float32) * (-2.0 * math.log(10000.0) / head_size))
    angle = position[:, None] * freq[None, :]
    cosine, sine = jnp.cos(angle), jnp.sin(angle)
    return (
        begin,
        jnp.concatenate([cosine, cosine], axis=1),
        jnp.concatenate([-sine, sine], axis=1),
    )


def spin(values, cosine, sine):
    return values * cosine + pltpu.roll(values, HD // 2, 1) * sine


def attend_kernel(
    q_ref, k_ref, v_ref, cq_ref, sq_ref, ck_ref, sk_ref, pq_ref, bq_ref, pk_ref,
    o_ref, lse_ref, saved_ref,
):
    step = pl.program_id(1)
    rows = q_ref.shape[0]
    factor = HD ** (-0.5) * math.log2(math.e)

    @pl.when(step == 0)
    def _():
        saved_ref[:, HD : 2 * HD] = spin(k_ref[...], ck_ref[...], sk_ref[...]).astype(jnp.bfloat16)
        saved_ref[:, 2 * HD :] = v_ref[...].astype(jnp.bfloat16)

    query = spin(q_ref[...], cq_ref[...], sq_ref[...]).astype(jnp.bfloat16)
    saved_ref[pl.ds(step * rows, rows), :HD] = query
    scores = lax.dot_general(
        query, saved_ref[:, HD : 2 * HD], (((1,), (1,)), ((), ())), preferred_element_type=jnp.float32
    )
    place = pk_ref[...]
    allowed = (place <= pq_ref[...]) & (place >= bq_ref[...])
    scores = jnp.where(allowed, scores * factor, NEG)
    top = jnp.max(scores, axis=1, keepdims=True)
    expo = jnp.exp2(scores - top)
    total = jnp.sum(expo, axis=1, keepdims=True)
    result = jnp.dot(
        expo.astype(jnp.bfloat16), saved_ref[:, 2 * HD :], preferred_element_type=jnp.float32
    )
    o_ref[...] = (result / total).astype(jnp.bfloat16)
    lse_ref[0] = top + jnp.log2(total)


def attend(joined, place, begin, cosine, sine):
    count = joined.shape[0]
    heads = joined.shape[1] // (3 * HD)
    cols = heads * HD
    rows = min(512, count)
    return pl.pallas_call(
        attend_kernel,
        name="attend",
        grid=(heads, count // rows),
        in_specs=[
            pl.BlockSpec((rows, HD), lambda h, i: (i, 3 * h)),
            pl.BlockSpec((count, HD), lambda h, i: (0, 3 * h + 1)),
            pl.BlockSpec((count, HD), lambda h, i: (0, 3 * h + 2)),
            pl.BlockSpec((rows, HD), lambda h, i: (i, 0)),
            pl.BlockSpec((rows, HD), lambda h, i: (i, 0)),
            pl.BlockSpec((count, HD), lambda h, i: (0, 0)),
            pl.BlockSpec((count, HD), lambda h, i: (0, 0)),
            pl.BlockSpec((rows, 1), lambda h, i: (i, 0)),
            pl.BlockSpec((rows, 1), lambda h, i: (i, 0)),
            pl.BlockSpec((1, count), lambda h, i: (0, 0)),
        ],
        out_specs=[
            pl.BlockSpec((rows, HD), lambda h, i: (i, h)),
            pl.BlockSpec((1, rows, 1), lambda h, i: (h, i, 0)),
            pl.BlockSpec((count, 3 * HD), lambda h, i: (0, h)),
        ],
        out_shape=[
            jax.ShapeDtypeStruct((count, cols), jnp.bfloat16),
            jax.ShapeDtypeStruct((heads, count, 1), jnp.float32),
            jax.ShapeDtypeStruct((count, 3 * cols), jnp.bfloat16),
        ],
        compiler_params=pltpu.CompilerParams(vmem_limit_bytes=56 * 1024 * 1024),
        cost_estimate=pl.CostEstimate(
            flops=4 * count * count * cols,
            transcendentals=heads * count * count,
            bytes_accessed=24 * count * cols,
        ),
    )(
        joined, joined, joined, cosine, sine, cosine, sine,
        place[:, None], begin[:, None], place[None, :],
    )


def attend_back_kernel(
    saved_q_ref, saved_k_ref, saved_v_ref, g_ref, lse_ref, cq_ref, sq_ref, ck_ref, sk_ref,
    pq_ref, bq_ref, pk_ref, out_ref, dk_ref, dv_ref,
):
    step = pl.program_id(1)
    rows = saved_q_ref.shape[0]
    scale = HD ** (-0.5)
    factor = scale * math.log2(math.e)

    @pl.when(step == 0)
    def _():
        dk_ref[...] = jnp.zeros_like(dk_ref)
        dv_ref[...] = jnp.zeros_like(dv_ref)

    query = saved_q_ref[...]
    keys = saved_k_ref[...]
    grad = g_ref[...]
    scores = lax.dot_general(
        query, keys, (((1,), (1,)), ((), ())), preferred_element_type=jnp.float32
    )
    place = pk_ref[...]
    allowed = (place <= pq_ref[...]) & (place >= bq_ref[...])
    probs = jnp.exp2(jnp.where(allowed, scores * factor, NEG) - lse_ref[0])
    grad_probs = lax.dot_general(
        grad, saved_v_ref[...], (((1,), (1,)), ((), ())), preferred_element_type=jnp.float32
    )
    product = probs * grad_probs
    delta = jnp.sum(product, axis=1, keepdims=True)
    grad_scores = (product - probs * delta).astype(jnp.bfloat16)
    dv_ref[...] += lax.dot_general(
        probs.astype(jnp.bfloat16), grad, (((0,), (0,)), ((), ())),
        preferred_element_type=jnp.float32,
    )
    dk_ref[...] += lax.dot_general(
        grad_scores, query, (((0,), (0,)), ((), ())), preferred_element_type=jnp.float32
    )
    grad_query = jnp.dot(grad_scores, keys, preferred_element_type=jnp.float32) * scale
    out_ref[pl.ds(step * rows, rows), :HD] = spin(
        grad_query, cq_ref[...], -sq_ref[...]
    ).astype(jnp.bfloat16)

    @pl.when(step == pl.num_programs(1) - 1)
    def _():
        grad_keys = spin(dk_ref[...] * scale, ck_ref[...], -sk_ref[...])
        out_ref[:, HD : 2 * HD] = grad_keys.astype(jnp.bfloat16)
        out_ref[:, 2 * HD :] = dv_ref[...].astype(jnp.bfloat16)


def attend_back(saved, grad, lse, place, begin, cosine, sine):
    count = saved.shape[0]
    heads = saved.shape[1] // (3 * HD)
    cols = heads * HD
    rows = min(512, count)
    return pl.pallas_call(
        attend_back_kernel,
        name="attend_back",
        grid=(heads, count // rows),
        in_specs=[
            pl.BlockSpec((rows, HD), lambda h, i: (i, 3 * h)),
            pl.BlockSpec((count, HD), lambda h, i: (0, 3 * h + 1)),
            pl.BlockSpec((count, HD), lambda h, i: (0, 3 * h + 2)),
            pl.BlockSpec((rows, HD), lambda h, i: (i, h)),
            pl.BlockSpec((1, rows, 1), lambda h, i: (h, i, 0)),
            pl.BlockSpec((rows, HD), lambda h, i: (i, 0)),
            pl.BlockSpec((rows, HD), lambda h, i: (i, 0)),
            pl.BlockSpec((count, HD), lambda h, i: (0, 0)),
            pl.BlockSpec((count, HD), lambda h, i: (0, 0)),
            pl.BlockSpec((rows, 1), lambda h, i: (i, 0)),
            pl.BlockSpec((rows, 1), lambda h, i: (i, 0)),
            pl.BlockSpec((1, count), lambda h, i: (0, 0)),
        ],
        out_specs=pl.BlockSpec((count, 3 * HD), lambda h, i: (0, h)),
        out_shape=jax.ShapeDtypeStruct((count, 3 * cols), jnp.bfloat16),
        scratch_shapes=[
            pltpu.VMEM((count, HD), jnp.float32),
            pltpu.VMEM((count, HD), jnp.float32),
        ],
        compiler_params=pltpu.CompilerParams(vmem_limit_bytes=56 * 1024 * 1024),
        cost_estimate=pl.CostEstimate(
            flops=10 * count * count * cols,
            transcendentals=heads * count * count,
            bytes_accessed=24 * count * cols,
        ),
    )(
        saved, saved, saved, grad, lse, cosine, sine, cosine, sine,
        place[:, None], begin[:, None], place[None, :],
    )


def send(values, pairs):
    return lax.ppermute(values, "tensor", pairs)


def up_pairs(low, high):
    return [(2 * z + c, 2 * z + 2 + c) for z in range(low, high) for c in range(2)]


def down_pairs(low, high):
    return [(2 * z + c, 2 * z - 2 + c) for z in range(low, high) for c in range(2)]


def partner_pairs(size):
    return [(t, t ^ 1) for t in range(size)]


def row_order(size, mode):
    if mode == "sc":
        return jnp.arange(size, dtype=jnp.int32)
    mine = lax.axis_index("tensor")
    chips = size // 2
    chip, core = mine // 2, mine % 2
    chip_of = (chip - jnp.arange(chips, dtype=jnp.int32)) % chips
    return jnp.concatenate([chip_of * 2 + core, chip_of * 2 + 1 - core])


def gather_rows(rows, size, mode):
    if mode == "sc":
        return lax.all_gather(rows, "tensor", axis=0, tiled=True)
    chips = size // 2
    chip = lax.axis_index("tensor") // 2
    up, down = {}, {}
    going_up = going_down = rows
    for s in range(1, chips):
        going_up = up[s] = send(going_up, up_pairs(s - 1, chips - 1))
        going_down = down[s] = send(going_down, down_pairs(1, chips - s + 1))
    mine = [rows]
    for s in range(1, chips):
        mine.append(jnp.where(chip >= s, up[s], down[chips - s]))
    other = [send(piece, partner_pairs(size)) for piece in mine]
    return jnp.concatenate(mine + other, axis=0)


def scatter_rows(make, count, size, mode):
    if mode == "sc":
        return lax.psum_scatter(
            make(0, count).astype(jnp.bfloat16), "tensor", scatter_dimension=0, tiled=True
        ).astype(jnp.float32)
    chips = size // 2
    half = count // 2
    each = half // chips
    given = send(make(half, count).astype(jnp.bfloat16), partner_pairs(size))
    mine = (make(0, half) + given.astype(jnp.float32)).astype(jnp.bfloat16)
    piece = [mine[s * each : (s + 1) * each] for s in range(chips)]
    up = down = None
    for t in range(1, chips):
        going_up, going_down = piece[t], piece[chips - t]
        if up is not None:
            going_up = (going_up.astype(jnp.float32) + up).astype(jnp.bfloat16)
            going_down = (going_down.astype(jnp.float32) + down).astype(jnp.bfloat16)
        up = send(going_up, up_pairs(0, t)).astype(jnp.float32)
        down = send(going_down, down_pairs(chips - t, chips)).astype(jnp.float32)
    return piece[0].astype(jnp.float32) + up + down


def fetch(weight, axis):
    return lax.all_gather(weight.astype(jnp.bfloat16), "dp", axis=axis, tiled=True)


def reduce_owned(term, axis):
    return lax.psum_scatter(
        term.astype(jnp.bfloat16), "dp", scatter_dimension=axis, tiled=True
    ).astype(jnp.float32)


def join_heads(weight):
    heads = weight.shape[2] // HD
    return jnp.concatenate(
        [weight[s, :, h * HD : (h + 1) * HD] for h in range(heads) for s in range(3)], axis=1
    )


def part_heads(joined):
    heads = joined.shape[1] // (3 * HD)
    return jnp.stack(
        [
            jnp.concatenate(
                [joined[:, (3 * h + s) * HD : (3 * h + s + 1) * HD] for h in range(heads)], axis=1
            )
            for s in range(3)
        ]
    )


def adamw(master, first, second, grad, rate):
    first_next = 0.5 * first + 0.5 * grad
    second_next = 0.5 * second + 0.5 * grad * grad
    master_next = master - rate * (first_next / (jnp.sqrt(second_next) + 1e-08) + 0.1 * master)
    return (grad, first_next, second_next, master_next)


def body(
    tokens,
    cotangent,
    lengths,
    places,
    owners,
    qkv_weight,
    qkv_first,
    qkv_second,
    out_weight,
    out_first,
    out_second,
    proj_weight,
    proj_first,
    proj_second,
    down_weight,
    down_first,
    down_second,
):
    f32, bf16 = jnp.float32, jnp.bfloat16
    groups = tokens.shape[0]
    each_rows = tokens.shape[1]
    count = places.shape[2]
    size = count // each_rows
    back_owners = [inverse_order(owners[i]) for i in range(4)]
    w_qkv = fetch(join_heads(qkv_weight), 0)
    w_out = fetch(out_weight, 1)
    w_proj = fetch(jnp.concatenate([proj_weight[0], proj_weight[1]], axis=1), 0)
    units = proj_weight.shape[2]
    w_down = fetch(down_weight, 1)
    modes = [ROW_COMM[m] for m in range(groups)]

    place, begin, cosine, sine = [], [], [], []
    rows_in, normed_one, scale_one, rows_a, grads_two = [], [], [], [], []
    for m in range(groups):
        arrival = inverse_order(places[m, 0])
        mine = jnp.take(
            arrival.reshape(size, each_rows), row_order(size, modes[m]), axis=0
        ).reshape(-1)
        first, cos, sin = layout(lengths[m, 0], mine, HD)
        place.append(mine)
        begin.append(first)
        cosine.append(cos)
        sine.append(sin)
        rows_in.append(tokens[m].astype(f32))
        normed, scale = normalize(rows_in[m])
        normed_one.append(normed)
        scale_one.append(scale)
        rows_a.append(gather_rows(pick_blocks(normed.astype(bf16), owners[0]), size, modes[m]))
    for m in range(groups):
        grads_two.append(gather_rows(pick_blocks(cotangent[m], owners[3]), size, modes[m]))

    outputs, input_grads = [], []
    total = None
    state = []
    for m in range(groups):
        joined = jnp.dot(rows_a[m], w_qkv, preferred_element_type=f32)
        attended, lse, saved = attend(joined, place[m], begin[m], cosine[m], sine[m])
        branch_one = scatter_rows(
            lambda low, high, attended=attended: jnp.dot(
                attended[low:high], w_out, preferred_element_type=f32
            ),
            count,
            size,
            modes[m],
        )
        middle = rows_in[m] + pick_blocks(branch_one, back_owners[1])
        normed_two, scale_two = normalize(middle)
        rows_b = gather_rows(pick_blocks(normed_two.astype(bf16), owners[2]), size, modes[m])
        gate_up = jnp.dot(rows_b, w_proj, preferred_element_type=f32)
        gate, up = gate_up[:, :units], gate_up[:, units:]
        sigma = jax.nn.sigmoid(gate)
        activated = gate * sigma
        hidden = (activated * up).astype(bf16)
        branch_two = scatter_rows(
            lambda low, high, hidden=hidden: jnp.dot(
                hidden[low:high], w_down, preferred_element_type=f32
            ),
            count,
            size,
            modes[m],
        )
        outputs.append((middle + pick_blocks(branch_two, back_owners[3])).astype(bf16))
        term_down = jnp.einsum("tf,td->fd", hidden, grads_two[m], preferred_element_type=f32)
        grad_hidden = jnp.einsum("td,fd->tf", grads_two[m], w_down, preferred_element_type=f32)
        grad_gate = grad_hidden * up * sigma * (1.0 + gate * (1.0 - sigma))
        grad_up = grad_hidden * activated
        grad_gate_up = jnp.concatenate([grad_gate.astype(bf16), grad_up.astype(bf16)], axis=1)
        term_proj = jnp.einsum("td,tf->df", rows_b, grad_gate_up, preferred_element_type=f32)
        grad_normed_two = pick_blocks(
            scatter_rows(
                lambda low, high, g=grad_gate_up: jnp.einsum(
                    "tf,df->td", g[low:high], w_proj, preferred_element_type=f32
                ),
                count,
                size,
                modes[m],
            ),
            back_owners[2],
        )
        grad_middle = cotangent[m].astype(f32) + normalize_back(
            normed_two, scale_two, grad_normed_two
        )
        grads_one = gather_rows(pick_blocks(grad_middle.astype(bf16), owners[1]), size, modes[m])
        term_out = jnp.einsum("tc,td->cd", attended, grads_one, preferred_element_type=f32)
        grad_attn = jnp.einsum("td,cd->tc", grads_one, w_out, preferred_element_type=f32)
        grad_joined = attend_back(
            saved, grad_attn.astype(bf16), lse, place[m], begin[m], cosine[m], sine[m]
        )
        term_qkv = jnp.einsum("td,tc->dc", rows_a[m], grad_joined, preferred_element_type=f32)
        grad_normed_one = pick_blocks(
            scatter_rows(
                lambda low, high, g=grad_joined: jnp.einsum(
                    "tc,dc->td", g[low:high], w_qkv, preferred_element_type=f32
                ),
                count,
                size,
                modes[m],
            ),
            back_owners[0],
        )
        input_grads.append(
            grad_middle + normalize_back(normed_one[m], scale_one[m], grad_normed_one)
        )
        terms = (term_qkv, term_out, term_proj, term_down)
        total = terms if total is None else tuple(a + b for a, b in zip(total, terms))
    down_new = adamw(down_weight, down_first, down_second, reduce_owned(total[3], 1), RATES[3])
    grad_proj = reduce_owned(total[2], 0)
    grad_proj = jnp.stack([grad_proj[:, :units], grad_proj[:, units:]])
    proj_new = adamw(proj_weight, proj_first, proj_second, grad_proj, RATES[2])
    out_new = adamw(out_weight, out_first, out_second, reduce_owned(total[1], 1), RATES[1])
    grad_qkv = part_heads(reduce_owned(total[0], 0))
    qkv_new = adamw(qkv_weight, qkv_first, qkv_second, grad_qkv, RATES[0])
    return (
        jnp.stack(outputs),
        jnp.stack(input_grads),
        *qkv_new,
        *out_new,
        *proj_new,
        *down_new,
    )


def solution(mesh):
    placed = (
        P(None, ("dp", "tensor"), None),
        P(None, ("dp", "tensor"), None),
        P(None, "dp", None),
        P(None, "dp", None),
        P(),
        P(None, "dp", "tensor"),
        P(None, "dp", "tensor"),
        P(None, "dp", "tensor"),
        P("tensor", "dp"),
        P("tensor", "dp"),
        P("tensor", "dp"),
        P(None, "dp", "tensor"),
        P(None, "dp", "tensor"),
        P(None, "dp", "tensor"),
        P("tensor", "dp"),
        P("tensor", "dp"),
        P("tensor", "dp"),
    )
    return jax.shard_map(
        body,
        mesh=mesh,
        in_specs=placed,
        out_specs=(
            P(None, ("dp", "tensor"), None),
            P(None, ("dp", "tensor"), None),
            P(None, "dp", "tensor"),
            P(None, "dp", "tensor"),
            P(None, "dp", "tensor"),
            P(None, "dp", "tensor"),
            P("tensor", "dp"),
            P("tensor", "dp"),
            P("tensor", "dp"),
            P("tensor", "dp"),
            P(None, "dp", "tensor"),
            P(None, "dp", "tensor"),
            P(None, "dp", "tensor"),
            P(None, "dp", "tensor"),
            P("tensor", "dp"),
            P("tensor", "dp"),
            P("tensor", "dp"),
            P("tensor", "dp"),
        ),
        check_vma=False,
    )
```
